32 devices in a mesh: dp: 8 (over z, x), tensor: 4 (over y, core).
Axes of the slice: x: 2, y: 2, z: 4, core: 2. Of those that a mesh axis runs over, the one named last changes fastest.
Arguments:
- inputs: bfloat16 [8192, 4096], P('dp'), may hold values from -6 to 6
- out_grads: bfloat16 [8192, 6144], P('dp', 'tensor'), may hold values from -0.01953125 to 0.01953125
- left_factor: float32 [4096, 4096], P('dp', 'tensor'), may hold values from -6 to 6
- right_factor: float32 [6144, 6144], P('dp', 'tensor'), may hold values from -6 to 6
- left_basis: float32 [4096, 4096], P('dp', 'tensor'), may hold values from -0.09375 to 0.09375
- right_basis: float32 [6144, 6144], P('dp', 'tensor'), may hold values from -0.078125 to 0.078125
Outputs:
- left_new: float32 [4096, 4096], P('dp', 'tensor')
- right_new: float32 [6144, 6144], P('dp', 'tensor')
- rotated: float32 [4096, 6144], P('dp', 'tensor')
The draws below stay inside these ranges and needn't reach their ends.
All inputs are finite; a program needn't handle non-finite values.
Results may differ from the reference program's by a relative error of at most 0.019.
Values may be sent and summed in bfloat16 or wider, within the bound.
A program may use at most 192 MiB of HBM per device.

```python
import jax
import jax.numpy as jnp
from jax import lax

M = 6144
K = 4096
TOK_DEV = 1024
TOKENS = 8192
N_DP = 8
N_TENSOR = 4


def steps_of(own_key, dims, cuts, low, high):
    factor_of, own = 1.0, jax.random.fold_in(own_key, 6)
    for axis_at, parts in cuts:
        draws = jnp.exp(jax.random.uniform(jax.random.fold_in(own, axis_at), (parts,), jnp.float32, low / len(cuts), high / len(cuts)))
        factor_of = factor_of * jnp.repeat(draws, dims[axis_at] // parts).reshape([-1 if axis == axis_at else 1 for axis in range(len(dims))])
    return factor_of


def centred(rng, extent, scale, reach, split=(), held_as=jnp.bfloat16):
    factor_of = steps_of(rng, extent, split, -0.22, 0.18) if split else 1.0
    drawn = jax.random.normal(rng, extent, jnp.float32) * scale * factor_of
    return jnp.minimum(jnp.maximum(drawn, -reach), reach).astype(held_as)


def setup_inputs(seed: int = 0) -> dict:
    streams_of = jax.random.split(jax.random.key(seed), 7)
    return {
        "inputs": centred(streams_of[0], (TOKENS, K), 1.0, 6.0, ((0, 8),)),
        "out_grads": centred(streams_of[1], (TOKENS, M), (TOKENS ** -0.5 * M ** -0.25), 0.01953125, ((0, 8), (1, 4))),
        "left_factor": centred(streams_of[2], (K, K), 1.0, 6.0, ((0, 8), (1, 4)), jnp.float32),
        "right_factor": centred(streams_of[3], (M, M), 1.0, 6.0, ((0, 8), (1, 4)), jnp.float32),
        "left_basis": centred(streams_of[4], (K, K), K ** -0.5, 0.09375, ((0, 8), (1, 4)), jnp.float32),
        "right_basis": centred(streams_of[5], (M, M), M ** -0.5, 0.078125, ((0, 8), (1, 4)), jnp.float32),
    }


def reference(inputs, out_grads, left_factor, right_factor, left_basis, right_basis):
    xs = inputs.reshape(N_DP, TOK_DEV, K)
    ys = out_grads.reshape(N_DP, TOK_DEV, M)

    def add_group(total, pair):
        part = jnp.dot(pair[0].T, pair[1], preferred_element_type=jnp.float32)
        return total + part.astype(jnp.bfloat16).astype(jnp.float32), None

    total, unused = lax.scan(add_group, jnp.zeros((K, M), jnp.float32), (xs, ys))
    grad = total.astype(jnp.bfloat16)

    cols = grad.reshape(K, N_TENSOR, M // N_TENSOR).transpose(1, 0, 2)

    def add_left(acc, panel):
        term = jnp.dot(panel, panel.T, preferred_element_type=jnp.float32)
        return acc + term.astype(jnp.bfloat16).astype(jnp.float32), None

    left_gram, unused = lax.scan(add_left, jnp.zeros((K, K), jnp.float32), cols)
    left_new = 0.95 * left_factor + 0.05 * left_gram

    rows = grad.reshape(N_DP, K // N_DP, M)

    def add_right(acc, panel):
        term = jnp.dot(panel.T, panel, preferred_element_type=jnp.float32)
        return acc + term.astype(jnp.bfloat16).astype(jnp.float32), None

    right_gram, unused = lax.scan(add_right, jnp.zeros((M, M), jnp.float32), rows)
    right_new = 0.95 * right_factor + 0.05 * right_gram

    left_low = left_basis.astype(jnp.bfloat16)
    right_low = right_basis.astype(jnp.bfloat16)
    turned = jnp.dot(grad, right_low, preferred_element_type=jnp.float32).astype(jnp.bfloat16)
    turned_rows = turned.reshape(N_DP, K // N_DP, M)
    basis_rows = left_low.reshape(N_DP, K // N_DP, K)

    def add_rot(acc, pair):
        term = jnp.dot(pair[0].T, pair[1], preferred_element_type=jnp.float32)
        return acc + term.astype(jnp.bfloat16).astype(jnp.float32), None

    rotated, unused = lax.scan(add_rot, jnp.zeros((K, M), jnp.float32), (basis_rows, turned_rows))
    return left_new, right_new, rotated
```

```python
import jax
import jax.numpy as jnp
from jax import lax
from jax.sharding import PartitionSpec as P

F32 = jnp.float32
BF16 = jnp.bfloat16


def mm(a, b, ca, cb):
    return lax.dot_general(a, b, (((ca,), (cb,)), ((), ())), preferred_element_type=F32)


def spread(block, owner, n_dp, n_t):
    me = lax.axis_index("tensor")
    mine = lax.rem(me - owner(lax.axis_index("dp")) + n_t, n_t)
    step = 1
    while step < n_t:
        pairs = []
        for d in range(n_dp):
            for k in range(step):
                if k + step < n_t:
                    src = (owner(d) + k) % n_t
                    dst = (owner(d) + k + step) % n_t
                    pairs.append((d * n_t + src, d * n_t + dst))
        got = lax.ppermute(block, ("dp", "tensor"), pairs)
        block = jnp.where((mine >= step) & (mine < 2 * step), got, block)
        step *= 2
    return block


def shards(inputs, out_grads, left_factor, right_factor, left_basis, right_basis):
    n_dp, n_t = lax.axis_size("dp"), lax.axis_size("tensor")
    krows, kcols = left_factor.shape
    mrows, mcols = right_factor.shape
    dp = lax.axis_index("dp")
    left_low = left_basis.astype(BF16)
    left_rows = lax.all_gather(left_low, "tensor", axis=1, tiled=True)
    left_cols = lax.all_to_all(left_rows, "dp", split_axis=1, concat_axis=0, tiled=True)
    basis_panel = lax.all_gather(right_basis.astype(BF16), "dp", axis=0, tiled=True)
    summed = lax.psum_scatter(
        mm(inputs, out_grads, 0, 0).astype(BF16), "dp", scatter_dimension=0, tiled=True
    )
    col_panel = lax.all_gather(summed, "dp", axis=0, tiled=True)
    turned = mm(left_cols, col_panel, 0, 0).astype(BF16)
    turned_rows = lax.all_gather(turned, "tensor", axis=1, tiled=True)
    own = lax.dynamic_slice_in_dim(col_panel, lax.rem(dp * mrows, mcols), mrows, 1)
    own = spread(own, lambda d: d * mrows // mcols, n_dp, n_t)
    parts = jnp.einsum(
        "jkc,rc->jrk", col_panel.reshape(n_t, kcols, mcols), summed, preferred_element_type=F32
    ).astype(BF16)
    gram_left = lax.psum_scatter(
        parts.reshape(n_t * krows, kcols), "tensor", scatter_dimension=0, tiled=True
    ).astype(F32)
    left_new = 0.95 * left_factor + 0.05 * gram_left
    right_new = 0.95 * right_factor + 0.05 * mm(own, col_panel, 0, 0)
    rotated = mm(turned_rows, basis_panel, 1, 0)
    return left_new, right_new, rotated


def solution(mesh):
    spec = P("dp", "tensor")
    return jax.shard_map(
        shards,
        mesh=mesh,
        in_specs=(P("dp", None), spec, spec, spec, spec, spec),
        out_specs=(spec, spec, spec),
        check_vma=False,
    )
```

```python
import jax
import jax.numpy as jnp
from jax import lax
from jax.sharding import PartitionSpec as P

F32 = jnp.float32
BF16 = jnp.bfloat16


def mm(a, b, ca, cb):
    return lax.dot_general(a, b, (((ca,), (cb,)), ((), ())), preferred_element_type=F32)


def spread(block, owner, n_dp, n_t, later):
    me = lax.axis_index("tensor")
    mine = me ^ owner(lax.axis_index("dp"))
    step = n_t // 2
    while step:
        pairs = []
        for d in range(n_dp):
            for k in range(0, n_t, 2 * step):
                src = owner(d) ^ k
                pairs.append((d * n_t + src, d * n_t + (src ^ step)))
        got = lax.ppermute(block, ("dp", "tensor"), pairs)
        if step == n_t // 2:
            got, later = lax.optimization_barrier((got, later))
        block = jnp.where(mine % (2 * step) == step, got, block)
        step //= 2
    return block, later


def gather_by_permutes(block, axis, n, hop):
    count = n // hop
    me = lax.axis_index(axis)
    group = me // hop
    got = [block]
    for r in range(1, count):
        pairs = [(p, (p // hop + r) % count * hop + p % hop) for p in range(n)]
        got.append(lax.ppermute(block, axis, pairs))
    return got, group, count


def in_order(got, group, count):
    out = jnp.zeros((count,) + got[0].shape, got[0].dtype)
    for r in range(count):
        out = lax.dynamic_update_slice_in_dim(out, got[r][None], lax.rem(group - r + count, count), 0)
    return out


def shards(inputs, out_grads, left_factor, right_factor, left_basis, right_basis):
    n_dp, n_t = lax.axis_size("dp"), lax.axis_size("tensor")
    krows, kcols = left_factor.shape
    mrows, mcols = right_factor.shape
    dp = lax.axis_index("dp")
    right_low = right_basis.astype(BF16)
    left_low = left_basis.astype(BF16)
    zgot, zgroup, zcount = gather_by_permutes(right_low, "dp", n_dp, 2)
    lgot, lgroup, lcount = gather_by_permutes(left_low, "tensor", n_t, 1)
    partial = mm(inputs, out_grads, 0, 0).astype(BF16)
    summed = lax.psum_scatter(partial, "dp", scatter_dimension=0, tiled=True)
    left_rows = in_order(lgot, lgroup, lcount)
    left_cols = lax.all_to_all(
        left_rows.reshape(n_t, krows, kcols // krows, krows).transpose(0, 2, 1, 3).reshape(n_dp, krows, krows),
        "dp", split_axis=0, concat_axis=0, tiled=True,
    ).reshape(n_dp * krows, krows)
    cross = [(p, p ^ 1) for p in range(n_dp)]
    early = len(zgot) // 2
    first = [lax.ppermute(z, "dp", cross) for z in zgot[:early]]
    summed, zgot, first, left_cols = lax.optimization_barrier((summed, zgot, first, left_cols))
    col_panel = lax.all_gather(summed, "dp", axis=0, tiled=True)
    last = [lax.ppermute(z, "dp", cross) for z in zgot[early:]]
    basis_panel = jnp.zeros((n_dp,) + right_low.shape, BF16)
    for r in range(early):
        at = lax.rem(zgroup - r + zcount, zcount) * 2 + lax.rem(dp, 2)
        basis_panel = lax.dynamic_update_slice_in_dim(basis_panel, zgot[r][None], at, 0)
        basis_panel = lax.dynamic_update_slice_in_dim(basis_panel, first[r][None], at ^ 1, 0)
    col_panel, last, basis_panel = lax.optimization_barrier((col_panel, last, basis_panel))
    for r in range(early, zcount):
        at = lax.rem(zgroup - r + zcount, zcount) * 2 + lax.rem(dp, 2)
        basis_panel = lax.dynamic_update_slice_in_dim(basis_panel, zgot[r][None], at, 0)
        basis_panel = lax.dynamic_update_slice_in_dim(basis_panel, last[r - early][None], at ^ 1, 0)
    basis_panel = basis_panel.reshape(n_dp * mrows, mcols)
    turned = mm(left_cols, col_panel, 0, 0).astype(BF16)
    turned, summed = lax.optimization_barrier((turned, summed))
    turned_rows = lax.all_gather(turned, "tensor", axis=1, tiled=True)
    own = lax.dynamic_slice_in_dim(col_panel, lax.rem(dp * mrows, mcols), mrows, 1)
    parts = jnp.einsum(
        "jkc,rc->jrk", col_panel.reshape(n_t, kcols, mcols), summed, preferred_element_type=F32
    ).astype(BF16)
    own, parts = spread(own, lambda d: d * mrows // mcols, n_dp, n_t, parts)
    gram_left = lax.psum_scatter(
        parts.reshape(n_t * krows, kcols), "tensor", scatter_dimension=0, tiled=True
    ).astype(F32)
    left_new = 0.95 * left_factor + 0.05 * gram_left
    right_new = 0.95 * right_factor + 0.05 * mm(own, col_panel, 0, 0)
    rotated = mm(turned_rows, basis_panel, 1, 0)
    return left_new, right_new, rotated


def solution(mesh):
    spec = P("dp", "tensor")
    return jax.shard_map(
        shards,
        mesh=mesh,
        in_specs=(P("dp", None), spec, spec, spec, spec, spec),
        out_specs=(spec, spec, spec),
        check_vma=False,
    )
```
